1024 devices in a mesh: ep: 64 (over z, y_lo), grp: 16 (over y_hi, x, core).
Axes of the slice: x: 4, y: 4 (y_hi: 2, y_lo: 2; y = y_hi * 2 + y_lo), z: 32, core: 2. Of those that a mesh axis runs over, the one named last changes fastest.
Arguments:
- tokens: bfloat16 [57344, 2048], P(('ep', 'grp')), may hold values from -6 to 6
- routes: int32 [57344, 3], P(('ep', 'grp')), may hold values from 0 to 63, all different within a row; in each aligned block of 56 rows (0 to 55, 56 to 111, ...) at most 3 rows name the same one
- combine: float32 [57344, 3], P(('ep', 'grp')), may hold values from 0.05 to 1
- cotangent: bfloat16 [57344, 2048], P(('ep', 'grp')), may hold values from -6 to 6
- w_in: bfloat16 [64, 2048, 768], P('ep'), may hold values from -0.125 to 0.125
- w_out: bfloat16 [64, 384, 2048], P('ep'), may hold values from -0.3125 to 0.3125
- mom_in: float32 [64, 2048, 768], P('ep', 'grp'), may hold values from -6 to 6
- var_in: float32 [64, 2048, 768], P('ep', 'grp'), may hold values from 0.1 to 10
- mom_out: float32 [64, 384, 2048], P('ep', None, 'grp'), may hold values from -6 to 6
- var_out: float32 [64, 384, 2048], P('ep', None, 'grp'), may hold values from 0.1 to 10
Outputs:
- token_grads: bfloat16 [57344, 2048], P(('ep', 'grp'))
- new_in: bfloat16 [64, 2048, 768], P('ep', 'grp')
- next_mom_in: float32 [64, 2048, 768], P('ep', 'grp')
- next_var_in: float32 [64, 2048, 768], P('ep', 'grp')
- new_out: bfloat16 [64, 384, 2048], P('ep', None, 'grp')
- next_mom_out: float32 [64, 384, 2048], P('ep', None, 'grp')
- next_var_out: float32 [64, 384, 2048], P('ep', None, 'grp')
The draws below stay inside these ranges and needn't reach their ends.
Inputs may be any that keep to these rules, and one draw needn't show every extreme that they name: `routes`: among the 56 tokens of one device no expert is named more than 3 times, and in every draw some expert is named exactly 3 times by some device; a token names 3 different experts.
All inputs are finite; a program needn't handle non-finite values.
Results may differ from the reference program's by a relative error of at most 0.022.
Values may be sent and summed in bfloat16 or wider, within the bound.
No kernel may reach another device: no remote copies, remote signals or barrier semaphores. Data moves between devices by JAX's collectives and lax.ppermute only.
A program may use at most 64 MiB of HBM per device.

```python
import math
import jax
import jax.numpy as jnp
import numpy as np
from jax import lax

D = 2048
HID = 384
TOPK = 3
TOK_DEV = 56
EXPERTS = 64
CAP = 3
TOKENS = 57344
N_EP = 64
N_GRP = 16


def shard_levels(rng, dims, cuts, smallest, largest):
    factor_of = 1.0
    for axis_at, shards_of in cuts:
        heights = jax.random.uniform(jax.random.fold_in(jax.random.fold_in(rng, 6), axis_at), (shards_of,), jnp.float32, smallest / len(cuts), largest / len(cuts))
        factor_of = factor_of * jnp.repeat(jnp.exp(heights), dims[axis_at] // shards_of).reshape((-1,) + (1,) * (len(dims) - 1 - axis_at))
    return factor_of


def shared_out(key, own, number, rows, amount, top, limit, lean):
    order = jax.random.permutation(key, amount)
    heavy_load, ordinary = load_shares(amount, rows * top, limit, lean, True), load_shares(amount, rows * top, limit, lean, False)
    places = jnp.arange(amount)

    def named(tallies, offset_by):
        used = int((tallies > 0).sum())
        fixed = max(1, used // 4)
        passed = fixed + (places - fixed + offset_by * (used - fixed)) % max(1, amount - fixed)
        return jnp.zeros((amount,), jnp.int32).at[order[jnp.where(places < fixed, places, passed)]].set(jnp.asarray(tallies, jnp.int32))

    tallies = jnp.where(number % 4 == 0, named(heavy_load, number // 4), named(ordinary, number - number // 4 - 1))
    mixed = jax.random.permutation(jax.random.fold_in(own, 3), amount)
    giver, taker = mixed[0:amount // 2 * 2:2], mixed[1:amount // 2 * 2:2]
    room = jnp.minimum(tallies[giver] - 1, limit - tallies[taker]) // 2
    room = jnp.where((giver == order[0]) | (taker == order[0]) | (tallies[taker] == 0), 0, jnp.maximum(room, 0))
    passed = jax.random.randint(jax.random.fold_in(own, 4), (amount // 2,), 0, 1 << 20) % (room + 1)
    tallies = tallies.at[giver].add(-passed).at[taker].add(passed)
    items = jnp.searchsorted(jnp.cumsum(tallies), jnp.arange(rows * top), side="right").astype(jnp.int32)
    grid = items.reshape(top, rows).T
    grid = grid[jax.random.permutation(jax.random.fold_in(own, 1), rows)]
    offset_by = jax.random.randint(jax.random.fold_in(own, 2), (rows, 1), 0, top)
    return jnp.take_along_axis(grid, (jnp.arange(top)[None, :] + offset_by) % top, axis=1)


def load_shares(amount, total, reach, skew, full):
    weights = [(1 << 20) // math.isqrt(grade ** skew) + 1 for grade in range(1, amount + 1)]
    largest = reach if full else min(reach, max(-(-total // amount), total * weights[0] // sum(weights)))
    least = 1 if total - largest >= amount - 1 else 0
    counts, spare = [largest] + [least] * (amount - 1), total - largest - least * (amount - 1)
    while spare > 0:
        free = [i for i in range(1, amount) if counts[i] < largest] or [i for i in range(1, amount) if counts[i] < reach]
        mass, budget = sum([weights[i] for i in free]), spare
        for i in free:
            more = min(reach - counts[i], max(1, budget * weights[i] // mass), spare)
            counts[i] = counts[i] + more
            spare = spare - more
    return np.array(counts)


def gaussian(stream_key, extent, spread, most, pieces=(), kind=jnp.bfloat16):
    array = jax.random.normal(stream_key, extent, jnp.float32) * spread
    if len(pieces) > 0:
        array = shard_levels(stream_key, extent, pieces, -0.22, 0.18) * array
    return jnp.clip(array, min=-most, max=most).astype(kind)


def setup_inputs(seed: int = 0) -> dict:
    arg_keys = jax.random.split(jax.random.key(seed), 11)
    tokens = gaussian(arg_keys[0], (TOKENS, D), 1.0, 6.0, ((0, 1024),))
    routes_keys = jax.random.split(jax.random.fold_in(arg_keys[1], 1), TOKENS // TOK_DEV)
    routes_turns = jax.random.permutation(jax.random.fold_in(arg_keys[1], 3), TOKENS // TOK_DEV)
    routes = jax.vmap(lambda own, number: shared_out(jax.random.fold_in(arg_keys[1], 2), own, number, TOK_DEV, EXPERTS, TOPK, CAP, 2))(routes_keys, routes_turns).reshape((TOKENS, TOPK))
    combine = jnp.clip(jnp.exp(math.log(1.0) - 2.9957323 * jax.random.uniform(arg_keys[2], (TOKENS, TOPK), jnp.float32) ** shard_levels(arg_keys[2], (TOKENS, TOPK), ((0, 1024),), -0.2, 0.2)), 0.05, 1.0)
    cotangent = gaussian(arg_keys[3], (TOKENS, D), 1.0, 6.0, ((0, 1024),))
    w_in = gaussian(arg_keys[4], (EXPERTS, D, 2 * HID), D ** -0.5, 0.125, ((0, 64),))
    w_out = gaussian(arg_keys[5], (EXPERTS, HID, D), HID ** -0.5, 0.3125, ((0, 64),))
    mom_in = gaussian(arg_keys[6], (EXPERTS, D, 2 * HID), 1.0, 6.0, ((0, 64), (1, 16)), jnp.float32)
    var_in = jnp.clip(jnp.exp(math.log(10.0) - 4.6051702 * jax.random.uniform(arg_keys[7], (EXPERTS, D, 2 * HID), jnp.float32) ** shard_levels(arg_keys[7], (EXPERTS, D, 2 * HID), ((0, 64), (1, 16)), -0.2, 0.2)), 0.1, 10.0)
    mom_out = gaussian(arg_keys[8], (EXPERTS, HID, D), 1.0, 6.0, ((0, 64), (2, 16)), jnp.float32)
    var_out = jnp.clip(jnp.exp(math.log(10.0) - 4.6051702 * jax.random.uniform(arg_keys[9], (EXPERTS, HID, D), jnp.float32) ** shard_levels(arg_keys[9], (EXPERTS, HID, D), ((0, 64), (2, 16)), -0.2, 0.2)), 0.1, 10.0)
    return {"tokens": tokens, "routes": routes, "combine": combine, "cotangent": cotangent, "w_in": w_in, "w_out": w_out, "mom_in": mom_in, "var_in": var_in, "mom_out": mom_out, "var_out": var_out}


beta_one = 0.9
beta_two = 0.95
learn_rate = 0.001
weight_decay = 0.1
epsilon = 1e-08
bias_one = 1.0 - 0.9 ** 10
bias_two = 1.0 - 0.95 ** 10

def adam_update(param, grad, moment, second):
    next_moment = beta_one * moment + (1.0 - beta_one) * grad
    next_second = beta_two * second + (1.0 - beta_two) * grad * grad
    step_size = next_moment / bias_one / (jnp.sqrt(next_second / bias_two) + epsilon)
    return ((param - learn_rate * (step_size + weight_decay * param)).astype(jnp.bfloat16), next_moment, next_second)

def group_sum(parts):
    rounded = parts.astype(jnp.bfloat16)
    rounded = lax.optimization_barrier(rounded)
    return lax.optimization_barrier(jnp.sum(rounded.astype(jnp.float32), axis=0))

def reference(tokens, routes, combine, cotangent, w_in, w_out, mom_in, var_in, mom_out, var_out):
    dev_count = TOKENS // TOK_DEV
    per_dev = TOK_DEV * TOPK
    total = TOKENS * TOPK
    flat_routes = routes.reshape(dev_count, per_dev).astype(jnp.int32)
    onehot = (flat_routes[:, :, None] == jnp.arange(EXPERTS, dtype=jnp.int32)[None, None, :]).astype(jnp.int32)
    slot_rank = lax.optimization_barrier(jnp.sum(jnp.cumsum(onehot, axis=1) * onehot, axis=2)) - 1
    dev_ids = jnp.broadcast_to(jnp.arange(dev_count, dtype=jnp.int32)[:, None], (dev_count, per_dev))
    row_ids = jnp.arange(total, dtype=jnp.int32).reshape(dev_count, per_dev)
    slot_table = jnp.full((EXPERTS, dev_count, CAP), total, jnp.int32)
    slot_table = slot_table.at[flat_routes, dev_ids, slot_rank].set(row_ids)
    slot_table = slot_table.reshape(EXPERTS, N_EP, N_GRP, CAP).transpose(0, 2, 1, 3)
    slot_table = slot_table.reshape(EXPERTS, N_GRP * N_EP * CAP)
    combine_flat = combine.reshape(total)

    def one_expert(grad_tokens, items):
        weight_in, weight_out, m_in, v_in, m_out, v_out, rows_of = items
        is_live = rows_of < total
        safe_rows = jnp.where(is_live, rows_of, 0)
        token_ids = safe_rows // TOPK
        inputs = jnp.where(is_live[:, None], tokens[token_ids], jnp.zeros((), jnp.bfloat16))
        weights_k = jnp.where(is_live, combine_flat[safe_rows], jnp.zeros((), jnp.float32))
        scaled = (weights_k[:, None] * cotangent[token_ids].astype(jnp.float32)).astype(jnp.bfloat16)
        pre = jnp.dot(inputs, weight_in, preferred_element_type=jnp.float32)
        gate_part = pre[:, :HID]
        up_part = pre[:, HID:]
        sig_gate = jax.nn.sigmoid(gate_part)
        active = gate_part * sig_gate
        hidden = (active * up_part).astype(jnp.bfloat16)
        d_hidden = jnp.dot(scaled, weight_out.T, preferred_element_type=jnp.float32)
        d_gate = d_hidden * up_part * (sig_gate * (1.0 + gate_part * (1.0 - sig_gate)))
        d_up = d_hidden * active
        d_pre = jnp.concatenate([d_gate, d_up], axis=1).astype(jnp.bfloat16)
        row_grad = jnp.dot(d_pre, weight_in.T, preferred_element_type=jnp.float32).astype(jnp.bfloat16)
        grad_tokens = grad_tokens.at[token_ids].add(jnp.where(is_live[:, None], row_grad.astype(jnp.float32), jnp.zeros((), jnp.float32)))
        rows_group = N_EP * CAP
        in_g = inputs.reshape(N_GRP, rows_group, D).astype(jnp.float32)
        pre_g = d_pre.reshape(N_GRP, rows_group, 2 * HID).astype(jnp.float32)
        hid_g = hidden.reshape(N_GRP, rows_group, HID).astype(jnp.float32)
        sca_g = scaled.reshape(N_GRP, rows_group, D).astype(jnp.float32)
        grad_in = group_sum(jnp.einsum('grd,grh->gdh', in_g, pre_g))
        grad_out = group_sum(jnp.einsum('grh,grd->ghd', hid_g, sca_g))
        new_a, mom_a, var_a = adam_update(weight_in.astype(jnp.float32), grad_in, m_in, v_in)
        new_b, mom_b, var_b = adam_update(weight_out.astype(jnp.float32), grad_out, m_out, v_out)
        return (grad_tokens, (new_a, mom_a, var_a, new_b, mom_b, var_b))
    start = jnp.zeros((TOKENS, D), jnp.float32)
    grad_tokens, results = lax.scan(one_expert, start, (w_in, w_out, mom_in, var_in, mom_out, var_out, slot_table))
    new_a, mom_a, var_a, new_b, mom_b, var_b = results
    return (grad_tokens.astype(jnp.bfloat16), new_a, mom_a, var_a, new_b, mom_b, var_b)
```

```python
import jax
import jax.numpy as jnp
from jax import lax
from jax.sharding import PartitionSpec as P

beta_one = 0.9
beta_two = 0.95
learn_rate = 0.001
weight_decay = 0.1
epsilon = 1e-08
bias_one = 1.0 - 0.9**10
bias_two = 1.0 - 0.95**10

LANES = 128
X_SIZE = 4
Y_SIZE = 2


def adam_update(param, grad, moment, second):
    next_moment = beta_one * moment + (1.0 - beta_one) * grad
    next_second = beta_two * second + (1.0 - beta_two) * grad * grad
    step_size = next_moment / bias_one / (jnp.sqrt(next_second / bias_two) + epsilon)
    return (
        (param - learn_rate * (step_size + weight_decay * param)).astype(jnp.bfloat16),
        next_moment,
        next_second,
    )


def exchange(rows, ep_count, capacity):
    slots, width = rows.shape
    packed = rows.reshape(ep_count, capacity, width // LANES, LANES)
    moved = lax.all_to_all(packed, "ep", split_axis=0, concat_axis=0, tiled=True)
    return moved.reshape(slots, width)


def tn_dot(left, right):
    return lax.dot_general(left, right, (((0,), (0,)), ((), ())), preferred_element_type=jnp.float32)


def nt_dot(left, right):
    return lax.dot_general(left, right, (((1,), (1,)), ((), ())), preferred_element_type=jnp.float32)


def per_device(tokens, routes, combine, cotangent, w_in, w_out, mom_in, var_in, mom_out, var_out):
    ep_count = lax.axis_size("ep")
    grp_count = lax.axis_size("grp")
    tok_rows, model_width = tokens.shape
    top_count = routes.shape[1]
    n_routed = tok_rows * top_count
    capacity = n_routed // ep_count + 1
    slot_count = ep_count * capacity
    weight_in = w_in[0]
    weight_out = w_out[0]
    hidden_width = weight_out.shape[0]
    me = lax.axis_index("grp")
    core = me & 1
    x_at = (me >> 1) & (X_SIZE - 1)
    y_at = me >> 3
    plane = X_SIZE * Y_SIZE
    share = model_width // grp_count

    flat_routes = routes.reshape(n_routed)
    onehot_int = (flat_routes[:, None] == jnp.arange(ep_count, dtype=jnp.int32)[None, :]).astype(
        jnp.int32
    )
    slot_rank = jnp.sum(jnp.cumsum(onehot_int, axis=0) * onehot_int, axis=1) - 1
    target = flat_routes * capacity + slot_rank
    placing = (jnp.arange(slot_count, dtype=jnp.int32)[:, None] == target[None, :]).astype(
        jnp.bfloat16
    )
    spread = placing.reshape(slot_count, tok_rows, top_count).sum(axis=2)
    scaled = (combine[:, :, None] * cotangent[:, None, :].astype(jnp.float32)).astype(jnp.bfloat16)
    scaled = scaled.reshape(n_routed, model_width)
    sent_rows = jnp.dot(spread, tokens, preferred_element_type=jnp.float32).astype(jnp.bfloat16)
    sent_grads = jnp.dot(placing, scaled, preferred_element_type=jnp.float32).astype(jnp.bfloat16)
    slot_inputs = exchange(sent_rows, ep_count, capacity)
    slot_grads = exchange(sent_grads, ep_count, capacity)

    pre = jnp.dot(slot_inputs, weight_in, preferred_element_type=jnp.float32)
    gate_part = pre[:, :hidden_width]
    up_part = pre[:, hidden_width:]
    sig_gate = jax.nn.sigmoid(gate_part)
    active = gate_part * sig_gate
    hidden = (active * up_part).astype(jnp.bfloat16)
    d_hidden = nt_dot(slot_grads, weight_out)
    d_gate = d_hidden * up_part * (sig_gate * (1.0 + gate_part * (1.0 - sig_gate)))
    d_up = d_hidden * active
    d_pre = jnp.concatenate([d_gate, d_up], axis=1).astype(jnp.bfloat16)
    row_grad = nt_dot(d_pre, weight_in).astype(jnp.bfloat16)
    back_rows = exchange(row_grad, ep_count, capacity)

    def of_core(rows, which):
        parts = rows.reshape(slot_count, plane, 2, share)
        return lax.dynamic_index_in_dim(parts, which, 2, keepdims=False).reshape(
            slot_count, plane * share
        )

    def grads_of(which):
        return (
            tn_dot(of_core(slot_inputs, which), d_pre),
            tn_dot(of_core(slot_grads, which), hidden),
        )

    swap = [(g, g ^ 1) for g in range(grp_count)]
    given = [lax.ppermute(g.astype(jnp.bfloat16), "grp", swap) for g in grads_of(1 - core)]
    kept = grads_of(core)
    chip = jnp.concatenate(
        [(a + b.astype(jnp.float32)).astype(jnp.bfloat16) for a, b in zip(kept, given)], axis=1
    )

    def block(dy, dx):
        at = (y_at ^ dy) * X_SIZE + ((x_at + dx) & (X_SIZE - 1))
        return lax.dynamic_slice_in_dim(chip, at * share, share, 0)

    def shifted(dy, dx):
        perm = []
        for g in range(grp_count):
            y, x, c = g // (2 * X_SIZE), (g // 2) % X_SIZE, g % 2
            perm.append((g, (((y + dy) % Y_SIZE) * X_SIZE + (x + dx) % X_SIZE) * 2 + c))
        return perm

    arrived = [block(0, 0)]
    for dy in range(Y_SIZE):
        for dx in range(X_SIZE):
            if (dy, dx) != (0, 0):
                arrived.append(lax.ppermute(block(dy, dx), "grp", shifted(dy, dx)))
    total = arrived[0].astype(jnp.float32)
    for part in arrived[1:]:
        total = total + part.astype(jnp.float32)
    grad_in = total[:, : 2 * hidden_width]
    grad_out = total[:, 2 * hidden_width :].T

    offset = me * share
    param_in = lax.dynamic_slice_in_dim(weight_in, offset, share, 0).astype(jnp.float32)
    param_out = lax.dynamic_slice_in_dim(weight_out, offset, share, 1).astype(jnp.float32)
    new_a, mom_a, var_a = adam_update(param_in, grad_in, mom_in[0], var_in[0])
    new_b, mom_b, var_b = adam_update(param_out, grad_out, mom_out[0], var_out[0])

    token_grads = tn_dot(spread, back_rows).astype(jnp.bfloat16)
    return (
        token_grads,
        new_a[None],
        mom_a[None],
        var_a[None],
        new_b[None],
        mom_b[None],
        var_b[None],
    )


def solution(mesh):
    return jax.shard_map(
        per_device,
        mesh=mesh,
        in_specs=(
            P(("ep", "grp"), None),
            P(("ep", "grp"), None),
            P(("ep", "grp"), None),
            P(("ep", "grp"), None),
            P("ep", None, None),
            P("ep", None, None),
            P("ep", "grp", None),
            P("ep", "grp", None),
            P("ep", None, "grp"),
            P("ep", None, "grp"),
        ),
        out_specs=(
            P(("ep", "grp"), None),
            P("ep", "grp", None),
            P("ep", "grp", None),
            P("ep", "grp", None),
            P("ep", None, "grp"),
            P("ep", None, "grp"),
            P("ep", None, "grp"),
        ),
        check_vma=False,
    )
```

```python
import functools

import jax
import jax.numpy as jnp
from jax import lax
from jax.experimental import pallas as pl
from jax.experimental.pallas import tpu as pltpu
from jax.sharding import PartitionSpec as P

beta_one = 0.9
beta_two = 0.95
learn_rate = 0.001
weight_decay = 0.1
epsilon = 1e-08
bias_one = 1.0 - 0.9**10
bias_two = 1.0 - 0.95**10

LANES = 128
X_SIZE = 4
Y_SIZE = 2


def adam_update(param, grad, moment, second):
    next_moment = beta_one * moment + (1.0 - beta_one) * grad
    next_second = beta_two * second + (1.0 - beta_two) * grad * grad
    step_size = next_moment / bias_one / (jnp.sqrt(next_second / bias_two) + epsilon)
    return (
        (param - learn_rate * (step_size + weight_decay * param)).astype(jnp.bfloat16),
        next_moment,
        next_second,
    )


def tn_dot(left, right):
    return lax.dot_general(left, right, (((0,), (0,)), ((), ())), preferred_element_type=jnp.float32)


def nt_dot(left, right):
    return lax.dot_general(left, right, (((1,), (1,)), ((), ())), preferred_element_type=jnp.float32)


def dispatch_kernel(capacity, routes_ref, combine_ref, tok_ref, cot_ref, out_ref, slot_ref, used_ref):
    experts = used_ref.shape[0]
    tok_rows, top_count = routes_ref.shape
    group = 2 * capacity

    def clear(e, carry):
        used_ref[e] = 0
        for c in range(group):
            out_ref[e * group + c] = jnp.zeros(out_ref.shape[1:], out_ref.dtype)
        return carry

    lax.fori_loop(0, experts, clear, 0)

    def place(t, carry):
        row = tok_ref[t]
        grad = cot_ref[t].astype(jnp.float32)
        for k in range(top_count):
            e = routes_ref[t, k]
            c = used_ref[e]
            used_ref[e] = c + 1
            at = e * group + c
            out_ref[at] = row
            out_ref[at + capacity] = (grad * combine_ref[t, k]).astype(out_ref.dtype)
            slot_ref[t, k] = e * capacity + c
        return carry

    lax.fori_loop(0, tok_rows, place, 0)


def dispatch(routes, combine, tokens, cotangent, experts, capacity):
    tok_rows, width = tokens.shape
    packed = (tok_rows, width // LANES, LANES)
    smem = pl.BlockSpec(memory_space=pltpu.SMEM)
    vmem = pl.BlockSpec(memory_space=pltpu.VMEM)
    rows = experts * 2 * capacity
    return pl.pallas_call(
        functools.partial(dispatch_kernel, capacity),
        out_shape=(
            jax.ShapeDtypeStruct((rows,) + packed[1:], tokens.dtype),
            jax.ShapeDtypeStruct(routes.shape, jnp.int32),
        ),
        in_specs=[smem, smem, vmem, vmem],
        out_specs=(vmem, smem),
        scratch_shapes=[pltpu.SMEM((experts,), jnp.int32)],
        name="dispatch",
    )(routes, combine, tokens.reshape(packed), cotangent.reshape(packed))


def block_grads(share, at, x_ref, s_ref, d_pre_ref, hidden_ref):
    cols = pl.ds(pl.multiple_of(at * share, share), share)
    return tn_dot(x_ref[:, cols], d_pre_ref[...]), tn_dot(s_ref[:, cols], hidden_ref[...])


def give_kernel(share, me_ref, x_ref, s_ref, d_pre_ref, hidden_ref, out_ref):
    other = 1 - (me_ref[0] & 1)
    wide = d_pre_ref.shape[1]
    for j in range(X_SIZE * Y_SIZE):
        a, b = block_grads(share, 2 * j + other, x_ref, s_ref, d_pre_ref, hidden_ref)
        out_ref[j * share : (j + 1) * share, :wide] = a.astype(out_ref.dtype)
        out_ref[j * share : (j + 1) * share, wide:] = b.astype(out_ref.dtype)


def keep_kernel(share, me_ref, x_ref, s_ref, d_pre_ref, hidden_ref, given_ref, *outs):
    me = me_ref[0]
    core, x_at, y_at = me & 1, (me >> 1) & (X_SIZE - 1), me >> 3
    wide = d_pre_ref.shape[1]
    for r, out_ref in enumerate(outs):
        j = (y_at ^ (r // X_SIZE)) * X_SIZE + ((x_at + r % X_SIZE) & (X_SIZE - 1))
        a, b = block_grads(share, 2 * j + core, x_ref, s_ref, d_pre_ref, hidden_ref)
        given = given_ref[pl.ds(pl.multiple_of(j * share, share), share), :].astype(jnp.float32)
        out_ref[:, :wide] = (a + given[:, :wide]).astype(out_ref.dtype)
        out_ref[:, wide:] = (b + given[:, wide:]).astype(out_ref.dtype)


def grads_call(kernel, share, out_shape, me, operands, name):
    vmem = pl.BlockSpec(memory_space=pltpu.VMEM)
    many = isinstance(out_shape, tuple)
    return pl.pallas_call(
        functools.partial(kernel, share),
        out_shape=out_shape,
        in_specs=[pl.BlockSpec(memory_space=pltpu.SMEM)] + [vmem] * len(operands),
        out_specs=(vmem,) * len(out_shape) if many else vmem,
        cost_estimate=pl.CostEstimate(flops=500_000_000, bytes_accessed=6_000_000, transcendentals=0),
        name=name,
    )(me, *operands)


def per_device(tokens, routes, combine, cotangent, w_in, w_out, mom_in, var_in, mom_out, var_out):
    ep_count = lax.axis_size("ep")
    grp_count = lax.axis_size("grp")
    tok_rows, model_width = tokens.shape
    top_count = routes.shape[1]
    capacity = tok_rows * top_count // ep_count + 1
    slot_count = ep_count * capacity
    lead = model_width // LANES
    weight_in = w_in[0]
    weight_out = w_out[0]
    hidden_width = weight_out.shape[0]
    me = lax.axis_index("grp")
    share = model_width // grp_count

    sent, slots = dispatch(routes, combine, tokens, cotangent, ep_count, capacity)
    sent = sent.reshape(ep_count, 2, capacity, lead, LANES)
    got = lax.all_to_all(sent, "ep", split_axis=0, concat_axis=0, tiled=True)
    slot_inputs = got[:, 0].reshape(slot_count, model_width)
    slot_grads = got[:, 1].reshape(slot_count, model_width)

    pre = jnp.dot(slot_inputs, weight_in, preferred_element_type=jnp.float32)
    gate_part = pre[:, :hidden_width]
    up_part = pre[:, hidden_width:]
    sig_gate = jax.nn.sigmoid(gate_part)
    active = gate_part * sig_gate
    hidden = (active * up_part).astype(jnp.bfloat16)
    d_hidden = nt_dot(slot_grads, weight_out)
    d_gate = d_hidden * up_part * (sig_gate * (1.0 + gate_part * (1.0 - sig_gate)))
    d_up = d_hidden * active
    d_pre = jnp.concatenate([d_gate, d_up], axis=1).astype(jnp.bfloat16)
    row_grad = nt_dot(d_pre, weight_in).astype(jnp.bfloat16)
    back = lax.all_to_all(
        row_grad.reshape(ep_count, capacity, lead, LANES), "ep", split_axis=0, concat_axis=0, tiled=True
    )

    me_ref = me.reshape(1)
    plane = X_SIZE * Y_SIZE
    wide = 3 * hidden_width
    operands = (slot_inputs, slot_grads, d_pre, hidden)
    swap = [(g, g ^ 1) for g in range(grp_count)]
    give = grads_call(
        give_kernel, share, jax.ShapeDtypeStruct((plane * share, wide), jnp.bfloat16), me_ref, operands, "give"
    )
    given = lax.ppermute(give, "grp", swap)
    block = jax.ShapeDtypeStruct((share, wide), jnp.bfloat16)
    blocks = grads_call(keep_kernel, share, (block,) * plane, me_ref, operands + (given,), "keep")

    def shifted(dy, dx):
        perm = []
        for g in range(grp_count):
            y, x, c = g // (2 * X_SIZE), (g // 2) % X_SIZE, g % 2
            perm.append((g, ((y ^ dy) * X_SIZE + (x + dx) % X_SIZE) * 2 + c))
        return perm

    total = blocks[0].astype(jnp.float32)
    for r in range(1, plane):
        moved = lax.ppermute(blocks[r], "grp", shifted(r // X_SIZE, r % X_SIZE))
        total = total + moved.astype(jnp.float32)
    grad_in = total[:, : 2 * hidden_width]
    grad_out = total[:, 2 * hidden_width :].T

    offset = me * share
    param_in = lax.dynamic_slice_in_dim(weight_in, offset, share, 0).astype(jnp.float32)
    param_out = lax.dynamic_slice_in_dim(weight_out, offset, share, 1).astype(jnp.float32)
    new_a, mom_a, var_a = adam_update(param_in, grad_in, mom_in[0], var_in[0])
    new_b, mom_b, var_b = adam_update(param_out, grad_out, mom_out[0], var_out[0])

    back_rows = back.reshape(slot_count, model_width)
    spread = jnp.zeros((slot_count, tok_rows), jnp.bool_)
    for k in range(top_count):
        spread = spread | (jnp.arange(slot_count, dtype=jnp.int32)[:, None] == slots[None, :, k])
    token_grads = tn_dot(spread.astype(jnp.bfloat16), back_rows).astype(jnp.bfloat16)
    return (
        token_grads,
        new_a[None],
        mom_a[None],
        var_a[None],
        new_b[None],
        mom_b[None],
        var_b[None],
    )


def solution(mesh):
    return jax.shard_map(
        per_device,
        mesh=mesh,
        in_specs=(
            P(("ep", "grp"), None),
            P(("ep", "grp"), None),
            P(("ep", "grp"), None),
            P(("ep", "grp"), None),
            P("ep", None, None),
            P("ep", None, None),
            P("ep", "grp", None),
            P("ep", "grp", None),
            P("ep", None, "grp"),
            P("ep", None, "grp"),
        ),
        out_specs=(
            P(("ep", "grp"), None),
            P("ep", "grp", None),
            P("ep", "grp", None),
            P("ep", "grp", None),
            P("ep", None, "grp"),
            P("ep", None, "grp"),
            P("ep", None, "grp"),
        ),
        check_vma=False,
    )
```

```python
import functools

import jax
import jax.numpy as jnp
from jax import lax
from jax.experimental import pallas as pl
from jax.experimental.pallas import tpu as pltpu
from jax.sharding import PartitionSpec as P

beta_one = 0.9
beta_two = 0.95
learn_rate = 0.001
weight_decay = 0.1
epsilon = 1e-08
bias_one = 1.0 - 0.9**10
bias_two = 1.0 - 0.95**10

LANES = 128
X_SIZE = 4
Y_SIZE = 2


def adam_update(param, grad, moment, second):
    next_moment = beta_one * moment + (1.0 - beta_one) * grad
    next_second = beta_two * second + (1.0 - beta_two) * grad * grad
    step_size = next_moment / bias_one / (jnp.sqrt(next_second / bias_two) + epsilon)
    return (
        (param - learn_rate * (step_size + weight_decay * param)).astype(jnp.bfloat16),
        next_moment,
        next_second,
    )


def tn_dot(left, right):
    return lax.dot_general(left, right, (((0,), (0,)), ((), ())), preferred_element_type=jnp.float32)


def nt_dot(left, right):
    return lax.dot_general(left, right, (((1,), (1,)), ((), ())), preferred_element_type=jnp.float32)


def dispatch_kernel(
    capacity, routes_ref, combine_ref, tokens_ref, cotangent_ref, out_ref, slot_ref, used_ref, tok_ref, cot_ref
):
    experts = used_ref.shape[0]
    top_count, tok_rows = routes_ref.shape
    group = 2 * capacity
    tok_ref[...] = tokens_ref[...].reshape(tok_ref.shape)
    cot_ref[...] = cotangent_ref[...].reshape(cot_ref.shape)

    def clear(e, carry):
        used_ref[e] = 0
        for c in range(group):
            out_ref[e * group + c] = jnp.zeros(out_ref.shape[1:], out_ref.dtype)
        return carry

    lax.fori_loop(0, experts, clear, 0, unroll=8)

    def place(t, carry):
        row = tok_ref[t]
        grad = cot_ref[t].astype(jnp.float32)
        for k in range(top_count):
            e = routes_ref[k, t]
            c = used_ref[e]
            used_ref[e] = c + 1
            at = e * group + c
            out_ref[at] = row
            out_ref[at + capacity] = (grad * combine_ref[k, t]).astype(out_ref.dtype)
            slot_ref[k, t] = e * capacity + c
        return carry

    lax.fori_loop(0, tok_rows, place, 0, unroll=8)


def dispatch(routes, combine, tokens, cotangent, experts, capacity):
    tok_rows, width = tokens.shape
    packed = (tok_rows, width // LANES, LANES)
    smem = pl.BlockSpec(memory_space=pltpu.SMEM)
    vmem = pl.BlockSpec(memory_space=pltpu.VMEM)
    rows = experts * 2 * capacity
    return pl.pallas_call(
        functools.partial(dispatch_kernel, capacity),
        out_shape=(
            jax.ShapeDtypeStruct((rows,) + packed[1:], tokens.dtype),
            jax.ShapeDtypeStruct(routes.shape, jnp.int32),
        ),
        in_specs=[smem, smem, vmem, vmem],
        out_specs=(vmem, smem),
        scratch_shapes=[
            pltpu.SMEM((experts,), jnp.int32),
            pltpu.VMEM(packed, tokens.dtype),
            pltpu.VMEM(packed, tokens.dtype),
        ],
        name="dispatch",
    )(routes, combine, tokens, cotangent)


def block_grads(share, at, x_ref, s_ref, d_pre_ref, hidden_ref):
    cols = pl.ds(pl.multiple_of(at * share, share), share)
    return tn_dot(x_ref[:, cols], d_pre_ref[...]), tn_dot(s_ref[:, cols], hidden_ref[...])


def give_kernel(share, me_ref, x_ref, s_ref, d_pre_ref, hidden_ref, out_ref):
    other = 1 - (me_ref[0] & 1)
    wide = d_pre_ref.shape[1]
    for j in range(X_SIZE * Y_SIZE):
        a, b = block_grads(share, 2 * j + other, x_ref, s_ref, d_pre_ref, hidden_ref)
        out_ref[j * share : (j + 1) * share, :wide] = a.astype(out_ref.dtype)
        out_ref[j * share : (j + 1) * share, wide:] = b.astype(out_ref.dtype)


def keep_kernel(share, me_ref, x_ref, s_ref, d_pre_ref, hidden_ref, given_ref, *outs):
    me = me_ref[0]
    core, x_at, y_at = me & 1, (me >> 1) & (X_SIZE - 1), me >> 3
    wide = d_pre_ref.shape[1]
    for r, out_ref in enumerate(outs):
        j = (y_at ^ (r // X_SIZE)) * X_SIZE + ((x_at + r % X_SIZE) & (X_SIZE - 1))
        a, b = block_grads(share, 2 * j + core, x_ref, s_ref, d_pre_ref, hidden_ref)
        given = given_ref[pl.ds(pl.multiple_of(j * share, share), share), :].astype(jnp.float32)
        out_ref[:, :wide] = (a + given[:, :wide]).astype(out_ref.dtype)
        out_ref[:, wide:] = (b + given[:, wide:]).astype(out_ref.dtype)


def grads_call(kernel, share, out_shape, me, operands, name):
    vmem = pl.BlockSpec(memory_space=pltpu.VMEM)
    many = isinstance(out_shape, tuple)
    return pl.pallas_call(
        functools.partial(kernel, share),
        out_shape=out_shape,
        in_specs=[pl.BlockSpec(memory_space=pltpu.SMEM)] + [vmem] * len(operands),
        out_specs=(vmem,) * len(out_shape) if many else vmem,
        cost_estimate=pl.CostEstimate(flops=500_000_000, bytes_accessed=6_000_000, transcendentals=0),
        name=name,
    )(me, *operands)


def per_device(tokens, routes, combine, cotangent, w_in, w_out, mom_in, var_in, mom_out, var_out):
    ep_count = lax.axis_size("ep")
    grp_count = lax.axis_size("grp")
    tok_rows, model_width = tokens.shape
    top_count = routes.shape[1]
    capacity = tok_rows * top_count // ep_count + 1
    slot_count = ep_count * capacity
    lead = model_width // LANES
    weight_in = w_in[0]
    weight_out = w_out[0]
    hidden_width = weight_out.shape[0]
    me = lax.axis_index("grp")
    share = model_width // grp_count

    sent, slots = dispatch(routes.T, combine.T, tokens, cotangent, ep_count, capacity)
    sent = sent.reshape(ep_count, 2, capacity, lead, LANES)
    got = lax.all_to_all(sent, "ep", split_axis=0, concat_axis=0, tiled=True)
    slot_inputs = got[:, 0].reshape(slot_count, model_width)
    slot_grads = got[:, 1].reshape(slot_count, model_width)

    pre = jnp.dot(slot_inputs, weight_in, preferred_element_type=jnp.float32)
    gate_part = pre[:, :hidden_width]
    up_part = pre[:, hidden_width:]
    sig_gate = jax.nn.sigmoid(gate_part)
    active = gate_part * sig_gate
    hidden = (active * up_part).astype(jnp.bfloat16)
    d_hidden = nt_dot(slot_grads, weight_out)
    d_gate = d_hidden * up_part * (sig_gate * (1.0 + gate_part * (1.0 - sig_gate)))
    d_up = d_hidden * active
    d_pre = jnp.concatenate([d_gate, d_up], axis=1).astype(jnp.bfloat16)
    row_grad = nt_dot(d_pre, weight_in).astype(jnp.bfloat16)
    back = lax.all_to_all(
        row_grad.reshape(ep_count, capacity, lead, LANES), "ep", split_axis=0, concat_axis=0, tiled=True
    )

    me_ref = me.reshape(1)
    plane = X_SIZE * Y_SIZE
    wide = 3 * hidden_width
    operands = (slot_inputs, slot_grads, d_pre, hidden)
    swap = [(g, g ^ 1) for g in range(grp_count)]
    give = grads_call(
        give_kernel, share, jax.ShapeDtypeStruct((plane * share, wide), jnp.bfloat16), me_ref, operands, "give"
    )
    given = lax.ppermute(give, "grp", swap)
    block = jax.ShapeDtypeStruct((share, wide), jnp.bfloat16)
    blocks = grads_call(keep_kernel, share, (block,) * plane, me_ref, operands + (given,), "keep")

    def shifted(dy, dx):
        perm = []
        for g in range(grp_count):
            y, x, c = g // (2 * X_SIZE), (g // 2) % X_SIZE, g % 2
            perm.append((g, ((y ^ dy) * X_SIZE + (x + dx) % X_SIZE) * 2 + c))
        return perm

    total = blocks[0].astype(jnp.float32)
    for r in range(1, plane):
        moved = lax.ppermute(blocks[r], "grp", shifted(r // X_SIZE, r % X_SIZE))
        total = total + moved.astype(jnp.float32)
    grad_in = total[:, : 2 * hidden_width]
    grad_out = total[:, 2 * hidden_width :].T

    offset = me * share
    param_in = lax.dynamic_slice_in_dim(weight_in, offset, share, 0).astype(jnp.float32)
    param_out = lax.dynamic_slice_in_dim(weight_out, offset, share, 1).astype(jnp.float32)
    new_a, mom_a, var_a = adam_update(param_in, grad_in, mom_in[0], var_in[0])
    new_b, mom_b, var_b = adam_update(param_out, grad_out, mom_out[0], var_out[0])

    back_rows = back.reshape(slot_count, model_width)
    spread = jnp.zeros((slot_count, tok_rows), jnp.bool_)
    for k in range(top_count):
        spread = spread | (jnp.arange(slot_count, dtype=jnp.int32)[:, None] == slots[k][None, :])
    token_grads = tn_dot(spread.astype(jnp.bfloat16), back_rows).astype(jnp.bfloat16)
    return (
        token_grads,
        new_a[None],
        mom_a[None],
        var_a[None],
        new_b[None],
        mom_b[None],
        var_b[None],
    )


def solution(mesh):
    return jax.shard_map(
        per_device,
        mesh=mesh,
        in_specs=(
            P(("ep", "grp"), None),
            P(("ep", "grp"), None),
            P(("ep", "grp"), None),
            P(("ep", "grp"), None),
            P("ep", None, None),
            P("ep", None, None),
            P("ep", "grp", None),
            P("ep", "grp", None),
            P("ep", None, "grp"),
            P("ep", None, "grp"),
        ),
        out_specs=(
            P(("ep", "grp"), None),
            P("ep", "grp", None),
            P("ep", "grp", None),
            P("ep", "grp", None),
            P("ep", None, "grp"),
            P("ep", None, "grp"),
            P("ep", None, "grp"),
        ),
        check_vma=False,
    )
```

```python
import functools

import jax
import jax.numpy as jnp
from jax import lax
from jax.experimental import pallas as pl
from jax.experimental.pallas import tpu as pltpu
from jax.sharding import PartitionSpec as P

beta_one = 0.9
beta_two = 0.95
learn_rate = 0.001
weight_decay = 0.1
epsilon = 1e-08
bias_one = 1.0 - 0.9**10
bias_two = 1.0 - 0.95**10

LANES = 128
X_SIZE = 4
Y_SIZE = 2


def adam_update(param, grad, moment, second):
    next_moment = beta_one * moment + (1.0 - beta_one) * grad
    next_second = beta_two * second + (1.0 - beta_two) * grad * grad
    step_size = next_moment / bias_one / (jnp.sqrt(next_second / bias_two) + epsilon)
    return (
        (param - learn_rate * (step_size + weight_decay * param)).astype(jnp.bfloat16),
        next_moment,
        next_second,
    )


def tn_dot(left, right):
    return lax.dot_general(left, right, (((0,), (0,)), ((), ())), preferred_element_type=jnp.float32)


def nt_dot(left, right):
    return lax.dot_general(left, right, (((1,), (1,)), ((), ())), preferred_element_type=jnp.float32)


def dispatch_kernel(
    capacity,
    routes_ref,
    combine_ref,
    tokens_ref,
    cotangent_ref,
    w_in_ref,
    w_out_ref,
    out_ref,
    slot_ref,
    near_in_ref,
    near_out_ref,
    used_ref,
    tok_ref,
    cot_ref,
    sems,
):
    fetch_in = pltpu.make_async_copy(w_in_ref.at[0], near_in_ref, sems.at[0])
    fetch_out = pltpu.make_async_copy(w_out_ref.at[0], near_out_ref, sems.at[1])
    fetch_in.start()
    fetch_out.start()
    experts = used_ref.shape[0]
    top_count, tok_rows = routes_ref.shape
    group = 2 * capacity
    tok_ref[...] = tokens_ref[...].reshape(tok_ref.shape)
    cot_ref[...] = cotangent_ref[...].reshape(cot_ref.shape)

    def clear(e, carry):
        used_ref[e] = 0
        for c in range(group):
            out_ref[e * group + c] = jnp.zeros(out_ref.shape[1:], out_ref.dtype)
        return carry

    lax.fori_loop(0, experts, clear, 0, unroll=8)

    def place(t, carry):
        row = tok_ref[t]
        grad = cot_ref[t].astype(jnp.float32)
        for k in range(top_count):
            e = routes_ref[k, t]
            c = used_ref[e]
            used_ref[e] = c + 1
            at = e * group + c
            out_ref[at] = row
            out_ref[at + capacity] = (grad * combine_ref[k, t]).astype(out_ref.dtype)
            slot_ref[k, t] = e * capacity + c
        return carry

    lax.fori_loop(0, tok_rows, place, 0, unroll=8)
    fetch_in.wait()
    fetch_out.wait()


def dispatch(routes, combine, tokens, cotangent, w_in, w_out, experts, capacity):
    tok_rows, width = tokens.shape
    packed = (tok_rows, width // LANES, LANES)
    smem = pl.BlockSpec(memory_space=pltpu.SMEM)
    vmem = pl.BlockSpec(memory_space=pltpu.VMEM)
    stay = pl.BlockSpec(memory_space=pl.ANY)
    rows = experts * 2 * capacity
    return pl.pallas_call(
        functools.partial(dispatch_kernel, capacity),
        out_shape=(
            jax.ShapeDtypeStruct((rows,) + packed[1:], tokens.dtype),
            jax.ShapeDtypeStruct(routes.shape, jnp.int32),
            pltpu.VMEM(w_in.shape[1:], w_in.dtype),
            pltpu.VMEM(w_out.shape[1:], w_out.dtype),
        ),
        in_specs=[smem, smem, vmem, vmem, stay, stay],
        out_specs=(vmem, smem, vmem, vmem),
        scratch_shapes=[
            pltpu.SMEM((experts,), jnp.int32),
            pltpu.VMEM(packed, tokens.dtype),
            pltpu.VMEM(packed, tokens.dtype),
            pltpu.SemaphoreType.DMA((2,)),
        ],
        compiler_params=pltpu.CompilerParams(vmem_limit_bytes=59 * 2**20),
        name="dispatch",
    )(routes, combine, tokens, cotangent, w_in, w_out)


def block_grads(share, at, x_ref, s_ref, d_pre_ref, hidden_ref):
    cols = pl.ds(pl.multiple_of(at * share, share), share)
    return tn_dot(x_ref[:, cols], d_pre_ref[...]), tn_dot(s_ref[:, cols], hidden_ref[...])


def give_kernel(share, me_ref, x_ref, s_ref, d_pre_ref, hidden_ref, out_ref):
    other = 1 - (me_ref[0] & 1)
    wide = d_pre_ref.shape[1]
    for j in range(X_SIZE * Y_SIZE):
        a, b = block_grads(share, 2 * j + other, x_ref, s_ref, d_pre_ref, hidden_ref)
        out_ref[j * share : (j + 1) * share, :wide] = a.astype(out_ref.dtype)
        out_ref[j * share : (j + 1) * share, wide:] = b.astype(out_ref.dtype)


def keep_kernel(share, me_ref, x_ref, s_ref, d_pre_ref, hidden_ref, given_ref, *outs):
    me = me_ref[0]
    core, x_at, y_at = me & 1, (me >> 1) & (X_SIZE - 1), me >> 3
    wide = d_pre_ref.shape[1]
    for r, out_ref in enumerate(outs):
        j = (y_at ^ (r // X_SIZE)) * X_SIZE + ((x_at + r % X_SIZE) & (X_SIZE - 1))
        a, b = block_grads(share, 2 * j + core, x_ref, s_ref, d_pre_ref, hidden_ref)
        given = given_ref[pl.ds(pl.multiple_of(j * share, share), share), :].astype(jnp.float32)
        out_ref[:, :wide] = (a + given[:, :wide]).astype(out_ref.dtype)
        out_ref[:, wide:] = (b + given[:, wide:]).astype(out_ref.dtype)


def grads_call(kernel, share, out_shape, me, operands, name):
    vmem = pl.BlockSpec(memory_space=pltpu.VMEM)
    many = isinstance(out_shape, tuple)
    return pl.pallas_call(
        functools.partial(kernel, share),
        out_shape=out_shape,
        in_specs=[pl.BlockSpec(memory_space=pltpu.SMEM)] + [vmem] * len(operands),
        out_specs=(vmem,) * len(out_shape) if many else vmem,
        cost_estimate=pl.CostEstimate(flops=500_000_000, bytes_accessed=6_000_000, transcendentals=0),
        name=name,
    )(me, *operands)


def per_device(tokens, routes, combine, cotangent, w_in, w_out, mom_in, var_in, mom_out, var_out):
    ep_count = lax.axis_size("ep")
    grp_count = lax.axis_size("grp")
    tok_rows, model_width = tokens.shape
    top_count = routes.shape[1]
    capacity = tok_rows * top_count // ep_count + 1
    slot_count = ep_count * capacity
    lead = model_width // LANES
    weight_in = w_in[0]
    weight_out = w_out[0]
    hidden_width = weight_out.shape[0]
    me = lax.axis_index("grp")
    share = model_width // grp_count

    sent, slots, near_in, near_out = dispatch(
        routes.T, combine.T, tokens, cotangent, w_in, w_out, ep_count, capacity
    )
    sent = sent.reshape(ep_count, 2, capacity, lead, LANES)
    got = lax.all_to_all(sent, "ep", split_axis=0, concat_axis=0, tiled=True)
    slot_inputs = got[:, 0].reshape(slot_count, model_width)
    slot_grads = got[:, 1].reshape(slot_count, model_width)

    pre = jnp.dot(slot_inputs, near_in, preferred_element_type=jnp.float32)
    gate_part = pre[:, :hidden_width]
    up_part = pre[:, hidden_width:]
    sig_gate = jax.nn.sigmoid(gate_part)
    active = gate_part * sig_gate
    hidden = (active * up_part).astype(jnp.bfloat16)
    d_hidden = nt_dot(slot_grads, near_out)
    d_gate = d_hidden * up_part * (sig_gate * (1.0 + gate_part * (1.0 - sig_gate)))
    d_up = d_hidden * active
    d_pre = jnp.concatenate([d_gate, d_up], axis=1).astype(jnp.bfloat16)
    row_grad = nt_dot(d_pre, near_in).astype(jnp.bfloat16)
    back = lax.all_to_all(
        row_grad.reshape(ep_count, capacity, lead, LANES), "ep", split_axis=0, concat_axis=0, tiled=True
    )

    me_ref = me.reshape(1)
    plane = X_SIZE * Y_SIZE
    wide = 3 * hidden_width
    operands = (slot_inputs, slot_grads, d_pre, hidden)
    swap = [(g, g ^ 1) for g in range(grp_count)]
    give = grads_call(
        give_kernel, share, jax.ShapeDtypeStruct((plane * share, wide), jnp.bfloat16), me_ref, operands, "give"
    )
    given = lax.ppermute(give, "grp", swap)
    block = jax.ShapeDtypeStruct((share, wide), jnp.bfloat16)
    blocks = grads_call(keep_kernel, share, (block,) * plane, me_ref, operands + (given,), "keep")

    def shifted(dy, dx):
        perm = []
        for g in range(grp_count):
            y, x, c = g // (2 * X_SIZE), (g // 2) % X_SIZE, g % 2
            perm.append((g, ((y ^ dy) * X_SIZE + (x + dx) % X_SIZE) * 2 + c))
        return perm

    total = blocks[0].astype(jnp.float32)
    for r in range(1, plane):
        moved = lax.ppermute(blocks[r], "grp", shifted(r // X_SIZE, r % X_SIZE))
        total = total + moved.astype(jnp.float32)
    grad_in = total[:, : 2 * hidden_width]
    grad_out = total[:, 2 * hidden_width :].T

    offset = me * share
    param_in = lax.dynamic_slice_in_dim(weight_in, offset, share, 0).astype(jnp.float32)
    param_out = lax.dynamic_slice_in_dim(weight_out, offset, share, 1).astype(jnp.float32)
    new_a, mom_a, var_a = adam_update(param_in, grad_in, mom_in[0], var_in[0])
    new_b, mom_b, var_b = adam_update(param_out, grad_out, mom_out[0], var_out[0])

    back_rows = back.reshape(slot_count, model_width)
    spread = jnp.zeros((slot_count, tok_rows), jnp.bool_)
    for k in range(top_count):
        spread = spread | (jnp.arange(slot_count, dtype=jnp.int32)[:, None] == slots[k][None, :])
    token_grads = tn_dot(spread.astype(jnp.bfloat16), back_rows).astype(jnp.bfloat16)
    return (
        token_grads,
        new_a[None],
        mom_a[None],
        var_a[None],
        new_b[None],
        mom_b[None],
        var_b[None],
    )


def solution(mesh):
    return jax.shard_map(
        per_device,
        mesh=mesh,
        in_specs=(
            P(("ep", "grp"), None),
            P(("ep", "grp"), None),
            P(("ep", "grp"), None),
            P(("ep", "grp"), None),
            P("ep", None, None),
            P("ep", None, None),
            P("ep", "grp", None),
            P("ep", "grp", None),
            P("ep", None, "grp"),
            P("ep", None, "grp"),
        ),
        out_specs=(
            P(("ep", "grp"), None),
            P("ep", "grp", None),
            P("ep", "grp", None),
            P("ep", "grp", None),
            P("ep", None, "grp"),
            P("ep", None, "grp"),
            P("ep", None, "grp"),
        ),
        check_vma=False,
    )
```

```python
import functools

import jax
import jax.numpy as jnp
from jax import lax
from jax.experimental import pallas as pl
from jax.experimental.pallas import tpu as pltpu
from jax.sharding import PartitionSpec as P

beta_one = 0.9
beta_two = 0.95
learn_rate = 0.001
weight_decay = 0.1
epsilon = 1e-08
bias_one = 1.0 - 0.9**10
bias_two = 1.0 - 0.95**10

LANES = 128
X_SIZE = 4
Y_SIZE = 2


def adam_update(param, grad, moment, second):
    next_moment = beta_one * moment + (1.0 - beta_one) * grad
    next_second = beta_two * second + (1.0 - beta_two) * grad * grad
    step_size = next_moment / bias_one / (jnp.sqrt(next_second / bias_two) + epsilon)
    return (
        (param - learn_rate * (step_size + weight_decay * param)).astype(jnp.bfloat16),
        next_moment,
        next_second,
    )


def tn_dot(left, right):
    return lax.dot_general(left, right, (((0,), (0,)), ((), ())), preferred_element_type=jnp.float32)


def nt_dot(left, right):
    return lax.dot_general(left, right, (((1,), (1,)), ((), ())), preferred_element_type=jnp.float32)


def dispatch_kernel(
    capacity,
    routes_ref,
    combine_ref,
    tokens_ref,
    cotangent_ref,
    w_in_ref,
    w_out_ref,
    out_ref,
    slot_ref,
    near_in_ref,
    near_out_ref,
    used_ref,
    tok_ref,
    cot_ref,
    flat_tok_ref,
    flat_cot_ref,
    sems,
):
    fetch_in = pltpu.make_async_copy(w_in_ref.at[0], near_in_ref, sems.at[0])
    fetch_out = pltpu.make_async_copy(w_out_ref.at[0], near_out_ref, sems.at[1])
    fetch_tok = pltpu.make_async_copy(tokens_ref, flat_tok_ref, sems.at[2])
    fetch_cot = pltpu.make_async_copy(cotangent_ref, flat_cot_ref, sems.at[3])
    for fetch in (fetch_tok, fetch_cot, fetch_in, fetch_out):
        fetch.start()
    experts = used_ref.shape[0]
    top_count, tok_rows = routes_ref.shape
    group = 2 * capacity
    def clear(e, carry):
        used_ref[e] = 0
        for c in range(group):
            out_ref[e * group + c] = jnp.zeros(out_ref.shape[1:], out_ref.dtype)
        return carry

    lax.fori_loop(0, experts, clear, 0, unroll=8)
    fetch_tok.wait()
    tok_ref[...] = flat_tok_ref[...].reshape(tok_ref.shape)
    fetch_cot.wait()
    cot_ref[...] = flat_cot_ref[...].reshape(cot_ref.shape)

    def place(t, carry):
        row = tok_ref[t]
        grad = cot_ref[t].astype(jnp.float32)
        for k in range(top_count):
            e = routes_ref[k, t]
            c = used_ref[e]
            used_ref[e] = c + 1
            at = e * group + c
            out_ref[at] = row
            out_ref[at + capacity] = (grad * combine_ref[k, t]).astype(out_ref.dtype)
            slot_ref[k, t] = e * capacity + c
        return carry

    lax.fori_loop(0, tok_rows, place, 0, unroll=8)
    fetch_in.wait()
    fetch_out.wait()


def dispatch(routes, combine, tokens, cotangent, w_in, w_out, experts, capacity):
    tok_rows, width = tokens.shape
    packed = (tok_rows, width // LANES, LANES)
    smem = pl.BlockSpec(memory_space=pltpu.SMEM)
    vmem = pl.BlockSpec(memory_space=pltpu.VMEM)
    stay = pl.BlockSpec(memory_space=pl.ANY)
    rows = experts * 2 * capacity
    return pl.pallas_call(
        functools.partial(dispatch_kernel, capacity),
        out_shape=(
            pltpu.VMEM((rows,) + packed[1:], tokens.dtype),
            jax.ShapeDtypeStruct(routes.shape, jnp.int32),
            pltpu.VMEM(w_in.shape[1:], w_in.dtype),
            pltpu.VMEM(w_out.shape[1:], w_out.dtype),
        ),
        in_specs=[smem, smem, stay, stay, stay, stay],
        out_specs=(vmem, smem, vmem, vmem),
        scratch_shapes=[
            pltpu.SMEM((experts,), jnp.int32),
            pltpu.VMEM(packed, tokens.dtype),
            pltpu.VMEM(packed, tokens.dtype),
            pltpu.VMEM(tokens.shape, tokens.dtype),
            pltpu.VMEM(tokens.shape, tokens.dtype),
            pltpu.SemaphoreType.DMA((4,)),
        ],
        compiler_params=pltpu.CompilerParams(vmem_limit_bytes=60_700_000),
        name="dispatch",
    )(routes, combine, tokens, cotangent, w_in, w_out)


def block_grads(share, at, x_ref, s_ref, d_pre_ref, hidden_ref):
    cols = pl.ds(pl.multiple_of(at * share, share), share)
    return tn_dot(x_ref[:, cols], d_pre_ref[...]), tn_dot(s_ref[:, cols], hidden_ref[...])


def give_kernel(share, me_ref, x_ref, s_ref, d_pre_ref, hidden_ref, out_ref):
    other = 1 - (me_ref[0] & 1)
    wide = d_pre_ref.shape[1]
    for j in range(X_SIZE * Y_SIZE):
        a, b = block_grads(share, 2 * j + other, x_ref, s_ref, d_pre_ref, hidden_ref)
        out_ref[j * share : (j + 1) * share, :wide] = a.astype(out_ref.dtype)
        out_ref[j * share : (j + 1) * share, wide:] = b.astype(out_ref.dtype)


def keep_kernel(share, me_ref, x_ref, s_ref, d_pre_ref, hidden_ref, given_ref, *outs):
    me = me_ref[0]
    core, x_at, y_at = me & 1, (me >> 1) & (X_SIZE - 1), me >> 3
    wide = d_pre_ref.shape[1]
    for r, out_ref in enumerate(outs):
        j = (y_at ^ (r // X_SIZE)) * X_SIZE + ((x_at + r % X_SIZE) & (X_SIZE - 1))
        a, b = block_grads(share, 2 * j + core, x_ref, s_ref, d_pre_ref, hidden_ref)
        given = given_ref[pl.ds(pl.multiple_of(j * share, share), share), :].astype(jnp.float32)
        out_ref[:, :wide] = (a + given[:, :wide]).astype(out_ref.dtype)
        out_ref[:, wide:] = (b + given[:, wide:]).astype(out_ref.dtype)


def grads_call(kernel, share, out_shape, me, operands, name):
    vmem = pl.BlockSpec(memory_space=pltpu.VMEM)
    many = isinstance(out_shape, tuple)
    return pl.pallas_call(
        functools.partial(kernel, share),
        out_shape=out_shape,
        in_specs=[pl.BlockSpec(memory_space=pltpu.SMEM)] + [vmem] * len(operands),
        out_specs=(vmem,) * len(out_shape) if many else vmem,
        cost_estimate=pl.CostEstimate(flops=500_000_000, bytes_accessed=6_000_000, transcendentals=0),
        name=name,
    )(me, *operands)


def per_device(tokens, routes, combine, cotangent, w_in, w_out, mom_in, var_in, mom_out, var_out):
    ep_count = lax.axis_size("ep")
    grp_count = lax.axis_size("grp")
    tok_rows, model_width = tokens.shape
    top_count = routes.shape[1]
    capacity = tok_rows * top_count // ep_count + 1
    slot_count = ep_count * capacity
    lead = model_width // LANES
    weight_in = w_in[0]
    weight_out = w_out[0]
    hidden_width = weight_out.shape[0]
    me = lax.axis_index("grp")
    share = model_width // grp_count

    sent, slots, near_in, near_out = dispatch(
        routes.T, combine.T, tokens, cotangent, w_in, w_out, ep_count, capacity
    )
    sent = sent.reshape(ep_count, 2, capacity, lead, LANES)
    got = lax.all_to_all(sent, "ep", split_axis=0, concat_axis=0, tiled=True)
    slot_inputs = got[:, 0].reshape(slot_count, model_width)
    slot_grads = got[:, 1].reshape(slot_count, model_width)

    pre = jnp.dot(slot_inputs, near_in, preferred_element_type=jnp.float32)
    gate_part = pre[:, :hidden_width]
    up_part = pre[:, hidden_width:]
    sig_gate = jax.nn.sigmoid(gate_part)
    active = gate_part * sig_gate
    hidden = (active * up_part).astype(jnp.bfloat16)
    d_hidden = nt_dot(slot_grads, near_out)
    d_gate = d_hidden * up_part * (sig_gate * (1.0 + gate_part * (1.0 - sig_gate)))
    d_up = d_hidden * active
    d_pre = jnp.concatenate([d_gate, d_up], axis=1).astype(jnp.bfloat16)
    row_grad = nt_dot(d_pre, near_in).astype(jnp.bfloat16)
    back = lax.all_to_all(
        row_grad.reshape(ep_count, capacity, lead, LANES), "ep", split_axis=0, concat_axis=0, tiled=True
    )

    me_ref = me.reshape(1)
    plane = X_SIZE * Y_SIZE
    wide = 3 * hidden_width
    operands = (slot_inputs, slot_grads, d_pre, hidden)
    swap = [(g, g ^ 1) for g in range(grp_count)]
    give = grads_call(
        give_kernel, share, jax.ShapeDtypeStruct((plane * share, wide), jnp.bfloat16), me_ref, operands, "give"
    )
    given = lax.ppermute(give, "grp", swap)
    block = jax.ShapeDtypeStruct((share, wide), jnp.bfloat16)
    blocks = grads_call(keep_kernel, share, (block,) * plane, me_ref, operands + (given,), "keep")

    def shifted(dy, dx):
        perm = []
        for g in range(grp_count):
            y, x, c = g // (2 * X_SIZE), (g // 2) % X_SIZE, g % 2
            perm.append((g, ((y ^ dy) * X_SIZE + (x + dx) % X_SIZE) * 2 + c))
        return perm

    total = blocks[0].astype(jnp.float32)
    for r in range(1, plane):
        moved = lax.ppermute(blocks[r], "grp", shifted(r // X_SIZE, r % X_SIZE))
        total = total + moved.astype(jnp.float32)
    grad_in = total[:, : 2 * hidden_width]
    grad_out = total[:, 2 * hidden_width :].T

    offset = me * share
    param_in = lax.dynamic_slice_in_dim(weight_in, offset, share, 0).astype(jnp.float32)
    param_out = lax.dynamic_slice_in_dim(weight_out, offset, share, 1).astype(jnp.float32)
    new_a, mom_a, var_a = adam_update(param_in, grad_in, mom_in[0], var_in[0])
    new_b, mom_b, var_b = adam_update(param_out, grad_out, mom_out[0], var_out[0])

    back_rows = back.reshape(slot_count, model_width)
    spread = jnp.zeros((slot_count, tok_rows), jnp.bool_)
    for k in range(top_count):
        spread = spread | (jnp.arange(slot_count, dtype=jnp.int32)[:, None] == slots[k][None, :])
    token_grads = tn_dot(spread.astype(jnp.bfloat16), back_rows).astype(jnp.bfloat16)
    return (
        token_grads,
        new_a[None],
        mom_a[None],
        var_a[None],
        new_b[None],
        mom_b[None],
        var_b[None],
    )


def solution(mesh):
    return jax.shard_map(
        per_device,
        mesh=mesh,
        in_specs=(
            P(("ep", "grp"), None),
            P(("ep", "grp"), None),
            P(("ep", "grp"), None),
            P(("ep", "grp"), None),
            P("ep", None, None),
            P("ep", None, None),
            P("ep", "grp", None),
            P("ep", "grp", None),
            P("ep", None, "grp"),
            P("ep", None, "grp"),
        ),
        out_specs=(
            P(("ep", "grp"), None),
            P("ep", "grp", None),
            P("ep", "grp", None),
            P("ep", "grp", None),
            P("ep", None, "grp"),
            P("ep", None, "grp"),
            P("ep", None, "grp"),
        ),
        check_vma=False,
    )
```
